32 devices in a mesh: inst: 8 (over z, y), space: 4 (over x, core).
Axes of the slice: x: 2, y: 2, z: 4, core: 2. Of those that a mesh axis runs over, the one named last changes fastest.
Arguments:
- state: float32 [32, 320, 512], P('inst', None, 'space'), may hold values from -6 to 6
- forcing: float32 [32, 320, 512], P('inst', None, 'space'), may hold values from -6 to 6
- flux_jac: float32 [3, 5, 5], replicated, may hold values from -0.875 to 0.875
- jacobi_inv: float32 [32, 320, 320], P('inst'), may hold values from -0.01 to 0.03
- cross_nbr: int32 [4, 64], replicated, may hold values from 0 to 63, as said below
- lower_match: int32 [32, 4, 64], P('inst', 'space'), may hold values from 0 to 63, as said below
Outputs:
- residual: float32 [32, 320, 512], P('inst', None, 'space')
- updated: float32 [32, 320, 512], P('inst', None, 'space')
The draws below stay inside these ranges and needn't reach their ends.
Inputs may be any that keep to these rules, and one draw needn't show every extreme that they name: `cross_nbr`: the cells form a grid of 8 by 8, periodic in both directions, in an order drawn from the seed; if row 0 names n for cell c then row 1 names c for n, and likewise rows 2 and 3. lower_match[t, p] is the identity except at the sliding interface p = 4 // 2, where it is the cyclic pitch shift of the cross_nbr grid by (t * 8 // 32 + r) % 8 rows, with one offset r drawn from the seed: the cell below that faces c is the one reached from c by that many steps through row 1 of cross_nbr.
All inputs are finite; a program needn't handle non-finite values.
Results may differ from the reference program's by a relative error of at most 0.0003.
Values sent between devices are 32-bit elements; how exact they have to be, the bound alone decides.
A program may use at most 128 MiB of HBM per device.

```python
import math
import jax
import jax.numpy as jnp
import numpy as np
from jax import lax

TIME_INSTANCES = 32
VARS = 5
NODE1 = 4
BLOCK = 320
EX = 2
PITCH_ELEMENTS = 8
EZ = 8
ELEMENTS = 512
SWEEPS = 2
N_SPACE = 4


def draw_jacobi_inv(key, part):
    noise = jnp.clip(jax.random.normal(key, (TIME_INSTANCES, BLOCK, BLOCK), jnp.float32), -4.0, 4.0)
    eye = jnp.eye(BLOCK, dtype=jnp.float32)
    base = 0.015 * eye[None] + 0.012 * noise / jnp.sqrt(jnp.float32(BLOCK))
    return base


def grid_order(key):
    cells = PITCH_ELEMENTS * EZ
    place = jax.random.permutation(jax.random.fold_in(key, 3), cells).astype(jnp.int32)
    owner = jnp.argsort(place).astype(jnp.int32)
    return (place, owner)


def draw_cross_nbr(key, part):
    place, owner = grid_order(key)
    row_pos = place // EZ
    col_pos = place % EZ
    minus_pitch = owner[(row_pos - 1) % PITCH_ELEMENTS * EZ + col_pos]
    plus_pitch = owner[(row_pos + 1) % PITCH_ELEMENTS * EZ + col_pos]
    minus_span = owner[row_pos * EZ + (col_pos - 1) % EZ]
    plus_span = owner[row_pos * EZ + (col_pos + 1) % EZ]
    return jnp.stack([minus_pitch, plus_pitch, minus_span, plus_span]).astype(jnp.int32)


def draw_lower_match(key, part):
    cells = PITCH_ELEMENTS * EZ
    place, owner = grid_order(key)
    row_pos = place // EZ
    col_pos = place % EZ
    pitch_offset = jax.random.randint(jax.random.fold_in(key, 11), (), 0, PITCH_ELEMENTS).astype(jnp.int32)
    period_samples = jnp.arange(TIME_INSTANCES, dtype=jnp.int32)
    phase_shifts = (period_samples * PITCH_ELEMENTS // TIME_INSTANCES + pitch_offset) % PITCH_ELEMENTS
    shifted = owner[(row_pos[None, :] + phase_shifts[:, None]) % PITCH_ELEMENTS * EZ + col_pos[None, :]].astype(jnp.int32)
    identity_map = jnp.broadcast_to(jnp.arange(cells, dtype=jnp.int32)[None, None, :], (TIME_INSTANCES, N_SPACE, cells))
    sliding = (jnp.arange(N_SPACE, dtype=jnp.int32) == N_SPACE // 2)[None, :, None]
    return jnp.where(sliding, shifted[:, None, :], identity_map).astype(jnp.int32)


def level_of(own_key, extent, cuts, low, top_value):
    factor_of, own = 1.0, jax.random.fold_in(own_key, 6)
    for position, shards_of in cuts:
        heights = jnp.exp(jax.random.uniform(jax.random.fold_in(own, position), (shards_of,), jnp.float32, low / len(cuts), top_value / len(cuts)))
        factor_of = factor_of * jnp.repeat(heights, extent[position] // shards_of).reshape([-1 if axis == position else 1 for axis in range(len(extent))])
    return factor_of


def bell_draw(stream_key, extent, scale, most, cuts=(), kind=jnp.bfloat16):
    drawn = scale * jax.random.normal(stream_key, extent, jnp.float32)
    if cuts:
        drawn = drawn * level_of(stream_key, extent, cuts, -0.22, 0.18)
    return jnp.clip(drawn, -most, most).astype(kind)


def setup_inputs(seed: int = 0) -> dict:
    keys = jax.random.split(jax.random.key(seed), 7)
    return {
        "state": bell_draw(keys[0], (TIME_INSTANCES, BLOCK, ELEMENTS), 1.0, 6.0, ((0, 8), (2, 4)), jnp.float32),
        "forcing": bell_draw(keys[1], (TIME_INSTANCES, BLOCK, ELEMENTS), 1.0, 6.0, ((0, 8), (2, 4)), jnp.float32),
        "flux_jac": bell_draw(keys[2], (3, VARS, VARS), (9 * VARS) ** -0.5, 0.875, (), jnp.float32),
        "jacobi_inv": draw_jacobi_inv(jax.random.fold_in(keys[6], 71), 0),
        "cross_nbr": draw_cross_nbr(jax.random.fold_in(keys[6], 71), 0),
        "lower_match": draw_lower_match(jax.random.fold_in(keys[6], 71), 0),
    }


dissipation = 0.6
frequency = 0.25

def lobatto_derivative(count_of_nodes):
    inner_point = math.sqrt(0.2)
    points = np.array([-1.0, -inner_point, inner_point, 1.0])
    barycentric = np.ones(count_of_nodes)
    for first_index in range(count_of_nodes):
        for second_index in range(count_of_nodes):
            if first_index != second_index:
                barycentric[first_index] = barycentric[first_index] / (points[first_index] - points[second_index])
    table = np.zeros((count_of_nodes, count_of_nodes))
    for first_index in range(count_of_nodes):
        for second_index in range(count_of_nodes):
            if first_index != second_index:
                table[first_index, second_index] = barycentric[second_index] / barycentric[first_index] / (points[first_index] - points[second_index])
        table[first_index, first_index] = -np.sum(table[first_index])
    return table

def surface_term(plus, minus, jacobian, sign):
    matrix = sign * jacobian - dissipation * jnp.eye(jacobian.shape[0], dtype=jnp.float32)
    return jnp.einsum('wv,vabg->wabg', matrix, plus - minus, precision=lax.Precision.HIGHEST)

def spatial_residual(field, flux_jac, derivative, cross_nbr, match):
    nodes = derivative.shape[0]
    width = flux_jac.shape[1]
    cells = cross_nbr.shape[1]
    total = field.shape[1]
    layers = total // cells
    highest = lax.Precision.HIGHEST
    reshaped_array = field.reshape(width, nodes, nodes, nodes, total)
    along_x = jnp.einsum('ai,vijkg->vajkg', derivative, reshaped_array, precision=highest)
    along_y = jnp.einsum('aj,vijkg->viakg', derivative, reshaped_array, precision=highest)
    along_z = jnp.einsum('ak,vijkg->vijag', derivative, reshaped_array, precision=highest)
    volume = jnp.einsum('wv,vijkg->wijkg', flux_jac[0], along_x, precision=highest)
    volume = volume + jnp.einsum('wv,vijkg->wijkg', flux_jac[1], along_y, precision=highest)
    volume = volume + jnp.einsum('wv,vijkg->wijkg', flux_jac[2], along_z, precision=highest)
    scale = nodes * (nodes - 1) / 4.0
    repeated = jnp.repeat(match, EX, axis=0).astype(jnp.int32)
    leading = (jnp.arange(layers) % EX == 0)[:, None]
    identity_map = jnp.arange(cells, dtype=jnp.int32)[None, :]
    full_map = jnp.where(leading, repeated, identity_map).astype(jnp.int32)
    inverse_map = jnp.argsort(full_map, axis=-1).astype(jnp.int32)
    low_x = reshaped_array[:, 0]
    high_x = reshaped_array[:, nodes - 1]
    split_low = low_x.reshape(width, nodes, nodes, layers, cells)
    split_high = high_x.reshape(width, nodes, nodes, layers, cells)
    empty_layer = jnp.zeros_like(split_high[:, :, :, :1])
    below = jnp.concatenate([empty_layer, split_high[:, :, :, :-1]], axis=3)
    below = jnp.take_along_axis(below, full_map[None, None, None], axis=4).reshape(width, nodes, nodes, total)
    above = jnp.take_along_axis(split_low, inverse_map[None, None, None], axis=4)
    above = jnp.concatenate([above[:, :, :, 1:], empty_layer], axis=3).reshape(width, nodes, nodes, total)
    low_y = reshaped_array[:, :, 0]
    high_y = reshaped_array[:, :, nodes - 1]
    low_z = reshaped_array[:, :, :, 0]
    high_z = reshaped_array[:, :, :, nodes - 1]

    def across(trace, face_row):
        split = trace.reshape(width, nodes, nodes, layers, cells)
        return jnp.take(split, cross_nbr[face_row], axis=4).reshape(width, nodes, nodes, total)
    volume = volume.at[:, 0].add(scale * surface_term(below, low_x, flux_jac[0], -1.0))
    volume = volume.at[:, nodes - 1].add(scale * surface_term(above, high_x, flux_jac[0], 1.0))
    volume = volume.at[:, :, 0].add(scale * surface_term(across(high_y, 0), low_y, flux_jac[1], -1.0))
    volume = volume.at[:, :, nodes - 1].add(scale * surface_term(across(low_y, 1), high_y, flux_jac[1], 1.0))
    volume = volume.at[:, :, :, 0].add(scale * surface_term(across(high_z, 2), low_z, flux_jac[2], -1.0))
    volume = volume.at[:, :, :, nodes - 1].add(scale * surface_term(across(low_z, 3), high_z, flux_jac[2], 1.0))
    return volume.reshape(field.shape[0], total)

def time_derivative(field):
    count = field.shape[0]
    spectrum = jnp.fft.rfft(field, axis=0)
    waves = jnp.arange(count // 2 + 1)
    factor = jnp.where(waves < count // 2, waves, 0) * frequency
    scaled = spectrum * (1j * factor)[:, None, None]
    return jnp.fft.irfft(scaled, n=count, axis=0).astype(jnp.float32)

def reference(state, forcing, flux_jac, jacobi_inv, cross_nbr, lower_match):
    derivative = jnp.asarray(lobatto_derivative(NODE1), jnp.float32)

    def instance_space(pieces):
        return spatial_residual(pieces[0], flux_jac, derivative, cross_nbr, pieces[1])

    def instance_update(pieces):
        return jnp.dot(pieces[0], pieces[1], preferred_element_type=jnp.float32, precision=lax.Precision.HIGHEST)
    current = state
    first_residual = state
    for sweep in range(SWEEPS):
        residual = lax.map(instance_space, (current, lower_match)) + time_derivative(current) - forcing
        if sweep == 0:
            first_residual = residual
        current = current - lax.map(instance_update, (jacobi_inv, residual))
    return (first_residual, current)
```

```python
import functools
import math

import jax
import jax.numpy as jnp
import numpy as np
from jax import lax
from jax.experimental import pallas as pl
from jax.experimental.pallas import tpu as pltpu
from jax.sharding import PartitionSpec as P

NODE1 = 4
SWEEPS = 2
DISSIPATION = 0.6
FREQUENCY = 0.25
LANES = 128
MESH = pl.DeviceIdType.MESH
BF = jnp.bfloat16
F32 = jnp.float32


def lobatto_derivative(count_of_nodes):
    inner_point = math.sqrt(0.2)
    points = np.array([-1.0, -inner_point, inner_point, 1.0])
    bary = np.ones(count_of_nodes)
    for a in range(count_of_nodes):
        for b in range(count_of_nodes):
            if a != b:
                bary[a] = bary[a] / (points[a] - points[b])
    table = np.zeros((count_of_nodes, count_of_nodes))
    for a in range(count_of_nodes):
        for b in range(count_of_nodes):
            if a != b:
                table[a, b] = bary[b] / bary[a] / (points[a] - points[b])
        table[a, a] = -np.sum(table[a])
    return table


def node_matrices():
    n = NODE1
    scale = n * (n - 1) / 4.0
    der = lobatto_derivative(n).astype(np.float32).astype(np.float64)
    eye = np.eye(n)
    low, high = np.zeros((n, n)), np.zeros((n, n))
    low[0, 0] = 1.0
    high[n - 1, n - 1] = 1.0
    to_low, to_high = np.zeros((n, n)), np.zeros((n, n))
    to_low[0, n - 1] = 1.0
    to_high[n - 1, 0] = 1.0

    def place(m, d):
        parts = [eye, eye, eye]
        parts[d] = m
        return np.kron(np.kron(parts[0], parts[1]), parts[2])

    own = [place(der + scale * (low - high), d) for d in range(3)]
    own.append(DISSIPATION * scale * sum(place(low + high, d) for d in range(3)))
    for d in range(3):
        own.append(place(scale * (to_high - to_low), d))
        own.append(-DISSIPATION * scale * place(to_high + to_low, d))
    return np.stack(own).astype(np.float32)


def time_weights(count):
    half = count // 2
    d = np.zeros(count)
    for m in range(1, count):
        d[m] = 0.5 * FREQUENCY * (-1.0) ** m / math.tan(math.pi * m / count)
    d[half] = 0.0
    plus = np.zeros((half, half))
    minus = np.zeros((half, half))
    for t in range(half):
        for s in range(half):
            a, b = d[(t - s) % count], d[(t - s + half) % count]
            plus[t, s] = 0.5 * (a + b)
            minus[t, s] = 0.5 * (a - b)
    return plus, minus


def split(x):
    hi = x.astype(BF)
    return hi, (x - hi.astype(F32)).astype(BF)


def mm(a, b):
    return jnp.dot(a, b, preferred_element_type=F32)


def kernel(
    cfg, flux, nodes, cross, match, state, forcing_hbm, jac_hbm, res_hbm, upd_hbm,
    xbuf, ybuf, dbuf, halo, match_up, v1, spat, forc, jac, jcat, vh, vl, wh, wl, py, pz, pb, pa,
    fsend, frecv, bsend, brecv, hsend, hrecv, msend, mrecv, lsem,
):
    n, ns, T, width, rows, chunks, crow, count, cells = cfg
    block = width * 64
    me = lax.axis_index("inst")
    sp = lax.axis_index("space")
    right, left = lax.rem(sp + 1, ns), lax.rem(sp + ns - 1, ns)
    peers = [lax.rem(me + k, n) for k in range(1, n)]

    load_f = pltpu.make_async_copy(forcing_hbm, forc, lsem.at[0])
    load_j = pltpu.make_async_copy(jac_hbm, jac, lsem.at[1])
    load_f.start()
    load_j.start()

    barrier = pltpu.get_barrier_semaphore()
    for p in peers:
        pl.semaphore_signal(barrier, inc=1, device_id={"inst": p}, device_id_type=MESH)
    for p in (right, left):
        pl.semaphore_signal(barrier, inc=1, device_id={"space": p}, device_id_type=MESH)
    pl.semaphore_wait(barrier, n + 1)

    padded = n * rows != block
    exact0 = state
    if padded:
        for t in range(T):
            v1[0, t, 0:block, :] = state[t]
            v1[0, t, block:, :] = jnp.zeros((n * rows - block, LANES), F32)
            v1[1, t, block:, :] = jnp.zeros((n * rows - block, LANES), F32)
        exact0 = v1.at[0]

    def forward(sweep, src, k, c):
        p = peers[k]
        return pltpu.make_async_remote_copy(
            src_ref=src.at[:, pl.ds(pl.multiple_of(p * rows + c * crow, 8), crow), :],
            dst_ref=xbuf.at[sweep, pl.ds(me * T, T), pl.ds(c * crow, crow), :],
            send_sem=fsend.at[sweep, k, c],
            recv_sem=frecv.at[sweep, k, c],
            device_id={"inst": p},
            device_id_type=MESH,
        )

    def backward(sweep, k, c):
        p = peers[k]
        return pltpu.make_async_remote_copy(
            src_ref=ybuf.at[sweep, pl.ds(p * T, T), pl.ds(c * crow, crow), :],
            dst_ref=dbuf.at[sweep, :, pl.ds(pl.multiple_of(me * rows + c * crow, 8), crow), :],
            send_sem=bsend.at[sweep, k, c],
            recv_sem=brecv.at[sweep, k, c],
            device_id={"inst": p},
            device_id_type=MESH,
        )

    def halos(sweep, src):
        out = []
        for t in range(T):
            for v in range(width):
                up = v * 64 + 48
                down = v * 64
                out.append(pltpu.make_async_remote_copy(
                    src_ref=src.at[t, pl.ds(up, 16), :],
                    dst_ref=halo.at[sweep, 0, t, pl.ds(v * 16, 16), :],
                    send_sem=hsend.at[sweep, 0, t * width + v],
                    recv_sem=hrecv.at[sweep, 0, t * width + v],
                    device_id={"space": right}, device_id_type=MESH))
                out.append(pltpu.make_async_remote_copy(
                    src_ref=src.at[t, pl.ds(down, 16), :],
                    dst_ref=halo.at[sweep, 1, t, pl.ds(v * 16, 16), :],
                    send_sem=hsend.at[sweep, 1, t * width + v],
                    recv_sem=hrecv.at[sweep, 1, t * width + v],
                    device_id={"space": left}, device_id_type=MESH))
        return out

    send_match = pltpu.make_async_remote_copy(
        src_ref=match, dst_ref=match_up, send_sem=msend.at[0], recv_sem=mrecv.at[0],
        device_id={"space": left}, device_id_type=MESH)

    plus, minus = time_weights(count)
    half = count // 2

    def derive(sweep, c):
        def group(g, _):
            at = pl.ds(pl.multiple_of(c * crow + g * 8, 8), 8)
            low = [xbuf[sweep, s, at, :] for s in range(half)]
            high = [xbuf[sweep, s + half, at, :] for s in range(half)]
            sums = [a + b for a, b in zip(low, high)]
            diffs = [a - b for a, b in zip(low, high)]
            for t in range(half):
                acc, dif = None, None
                for s in range(half):
                    if abs(plus[t, s]) > 1e-12:
                        term = sums[s] * float(plus[t, s])
                        acc = term if acc is None else acc + term
                    if abs(minus[t, s]) > 1e-12:
                        term = diffs[s] * float(minus[t, s])
                        dif = term if dif is None else dif + term
                ybuf[sweep, t, at, :] = acc + dif
                ybuf[sweep, t + half, at, :] = acc - dif
            return 0
        lax.fori_loop(0, crow // 8, group, 0)

    src_row = lax.broadcasted_iota(jnp.int32, (LANES, LANES), 0)
    dst_col = lax.broadcasted_iota(jnp.int32, (LANES, LANES), 1)

    def onehot(mask):
        return jnp.where(mask, 1.0, 0.0).astype(F32)

    def build_weights():
        lane_var = lax.broadcasted_iota(jnp.int32, (1, block), 1) // 64
        tiles = [jnp.concatenate([nodes[i]] * width, axis=1) for i in range(10)]
        for w in range(width):
            fe = []
            for d in range(3):
                row = jnp.zeros((1, block), F32)
                for v in range(width):
                    row = jnp.where(lane_var == v, flux[d, w, v], row)
                fe.append(row)
            same = jnp.where(lane_var == w, 1.0, 0.0)
            parts = [fe[0] * tiles[0] + fe[1] * tiles[1] + fe[2] * tiles[2] + same * tiles[3]]
            for d in range(3):
                parts.append(fe[d] * tiles[4 + 2 * d] + same * tiles[5 + 2 * d])
            hi, lo = split(jnp.concatenate(parts, axis=1))
            wh[w * 64:(w + 1) * 64, :] = hi
            wl[w * 64:(w + 1) * 64, :] = lo

    def build_moves():
        layer = (lax.broadcasted_iota(jnp.int32, (1, LANES), 1) // cells) * cells
        for f in range(4):
            nb = cross[f:f + 1, :]
            nb = jnp.concatenate([nb] * (LANES // cells), axis=1) + layer
            ref = py if f < 2 else pz
            ref[(f % 2) * LANES:(f % 2 + 1) * LANES, :] = onehot(src_row == nb).astype(BF)

    def build_match():
        last = LANES - cells
        low_ok = jnp.where(sp > 0, 1.0, 0.0)
        high_ok = jnp.where(sp < ns - 1, 1.0, 0.0)
        shift_up = onehot(dst_col == src_row + cells).astype(BF)
        shift_down = onehot(src_row == dst_col + cells).astype(BF)
        for t in range(T):
            m = jnp.concatenate([match[t]] * (LANES // cells), axis=1)
            mu = jnp.concatenate([match_up[t]] * (LANES // cells), axis=1)
            pb[t, 0:LANES, :] = shift_up
            pb[t, LANES:, :] = (onehot((dst_col < cells) & (src_row == m + last)) * low_ok).astype(BF)
            pa[t, 0:LANES, :] = shift_down
            turned = onehot((dst_col < cells) & (src_row == mu + last)) * high_ok
            pa[t, LANES:, :] = turned.T.astype(BF)

    row_id = lax.broadcasted_iota(jnp.int32, (block, 1), 0)

    def as_mask(index, value):
        return jnp.where(index == value, 1.0, 0.0).astype(F32)

    mj3, mj0 = as_mask((row_id >> 2) & 3, 3), as_mask((row_id >> 2) & 3, 0)
    mk3, mk0 = as_mask(row_id & 3, 3), as_mask(row_id & 3, 0)

    def spread_cross(src, t):
        cols = slice(t * LANES, (t + 1) * LANES)
        x = src[t, 0:block, :]
        for part, out in zip(split(x), (vh, vl)):
            out[0:block, cols] = part
            wide = part.astype(F32)
            y = jnp.concatenate([wide * mj3, wide * mj0], axis=1).astype(BF)
            z = jnp.concatenate([wide * mk3, wide * mk0], axis=1).astype(BF)
            out[2 * block:3 * block, cols] = mm(y, py[...]).astype(BF)
            out[3 * block:4 * block, cols] = mm(z, pz[...]).astype(BF)

    def spread_flow(sweep, src, t):
        cols = slice(t * LANES, (t + 1) * LANES)
        own_high = jnp.concatenate([src[t, v * 64 + 48:v * 64 + 64, :] for v in range(width)], axis=0)
        own_low = jnp.concatenate([src[t, v * 64:v * 64 + 16, :] for v in range(width)], axis=0)
        high = split(jnp.concatenate([own_high, halo[sweep, 0, t]], axis=1))
        low = split(jnp.concatenate([own_low, halo[sweep, 1, t]], axis=1))
        for i, out in enumerate((vh, vl)):
            ub = mm(high[i], pb[t]).astype(BF)
            ua = mm(low[i], pa[t]).astype(BF)
            for v in range(width):
                base = block + v * 64
                out[base:base + 16, cols] = ua[v * 16:(v + 1) * 16]
                out[base + 48:base + 64, cols] = ub[v * 16:(v + 1) * 16]

    def clear_middle():
        for out in (vh, vl):
            for v in range(width):
                base = block + v * 64 + 16
                out[base:base + 32, :] = jnp.zeros((32, T * LANES), BF)

    def split_jac():
        load_j.wait()
        for t in range(T):
            hi, lo = split(jac[t])
            jcat[t] = jnp.concatenate([hi, lo, hi], axis=1)

    def apply_space():
        total = mm(wh[...], vh[...]) + mm(wl[...], vh[...]) + mm(wh[...], vl[...])
        for t in range(T):
            spat[t] = total[:, t * LANES:(t + 1) * LANES] - forc[t]

    own_rows = pl.ds(pl.multiple_of(me * rows, 8), rows)
    own_times = pl.ds(me * T, T)

    def run_sweep(sweep, src, setup):
        jobs = list(setup)
        per = -(-len(jobs) // chunks)
        xbuf[sweep, own_times, :, :] = src[:, own_rows, :]
        for c in range(chunks):
            for job in jobs[c * per:(c + 1) * per]:
                job()
            for k in range(n - 1):
                forward(sweep, src, k, c).wait_recv()
            derive(sweep, c)
            for k in range(n - 1):
                backward(sweep, k, c).start()
        dbuf[sweep, :, own_rows, :] = ybuf[sweep, own_times, :, :]

    def finish(sweep, src, dst):
        for c in range(chunks):
            for k in range(n - 1):
                backward(sweep, k, c).wait_recv()
        for t in range(T):
            r = spat[t] + dbuf[sweep, t, 0:block, :]
            if sweep == 0:
                spat[t] = r
            hi, lo = split(r)
            step = mm(jcat[t], jnp.concatenate([hi, hi, lo], axis=0))
            dst[t, 0:block, :] = src[t, 0:block, :] - step

    for c in range(chunks):
        for k in range(n - 1):
            forward(0, exact0, k, c).start()
    first_halos = halos(0, state)
    send_match.start()
    for h in first_halos:
        h.start()

    def wait_halos(sweep, src):
        for h in halos(sweep, src):
            h.wait_recv()

    def first_halo_ready():
        send_match.wait()
        wait_halos(0, state)
        build_match()

    setup0 = [build_moves, build_weights]
    setup0 += [functools.partial(spread_cross, state, t) for t in range(T)]
    setup0 += [clear_middle, first_halo_ready]
    setup0 += [functools.partial(spread_flow, 0, state, t) for t in range(T)]
    setup0 += [split_jac]
    run_sweep(0, exact0, setup0)
    load_f.wait()
    apply_space()
    cur = v1.at[1]
    finish(0, state, cur)

    for c in range(chunks):
        for k in range(n - 1):
            forward(1, cur, k, c).start()
    for h in halos(1, cur):
        h.start()
    store_r = pltpu.make_async_copy(spat, res_hbm, lsem.at[2])
    store_r.start()
    setup1 = [functools.partial(spread_cross, cur, t) for t in range(T)]
    setup1 += [functools.partial(wait_halos, 1, cur)]
    setup1 += [functools.partial(spread_flow, 1, cur, t) for t in range(T)]
    run_sweep(1, cur, setup1)
    store_r.wait()
    apply_space()
    finish(1, cur, forc)
    store_u = pltpu.make_async_copy(forc, upd_hbm, lsem.at[3])
    store_u.start()
    for sweep, src in ((0, exact0), (1, cur)):
        for c in range(chunks):
            for k in range(n - 1):
                forward(sweep, src, k, c).wait_send()
                backward(sweep, k, c).wait_send()
        for h in halos(sweep, state if sweep == 0 else cur):
            h.wait_send()
    store_u.wait()


def body(n, ns, state, forcing, flux_jac, jacobi_inv, cross_nbr, lower_match):
    T, block, elements = state.shape
    width = flux_jac.shape[1]
    cells = cross_nbr.shape[1]
    count = n * T
    rows = -(-block // (8 * n)) * 8
    crow = 8
    chunks = rows // crow
    halo_rows = width * 16
    cfg = (n, ns, T, width, rows, chunks, crow, count, cells)
    full = n * rows
    dma = pltpu.SemaphoreType.DMA
    vmem = pl.BlockSpec(memory_space=pltpu.VMEM)
    hbm = pl.BlockSpec(memory_space=pl.ANY)
    out = jax.ShapeDtypeStruct(state.shape, F32)
    return pl.pallas_call(
        functools.partial(kernel, cfg),
        name="sweeps",
        out_shape=(out, out),
        in_specs=[pl.BlockSpec(memory_space=pltpu.SMEM), vmem, vmem, vmem, vmem, hbm, hbm],
        out_specs=(hbm, hbm),
        scratch_shapes=[
            pltpu.VMEM((SWEEPS, count, rows, LANES), F32),
            pltpu.VMEM((SWEEPS, count, rows, LANES), F32),
            pltpu.VMEM((SWEEPS, T, full, LANES), F32),
            pltpu.VMEM((SWEEPS, 2, T, halo_rows, LANES), F32),
            pltpu.VMEM((T, 1, cells), jnp.int32),
            pltpu.VMEM((2, T, full, LANES), F32),
            pltpu.VMEM((T, block, LANES), F32),
            pltpu.VMEM((T, block, LANES), F32),
            pltpu.VMEM((T, block, block), F32),
            pltpu.VMEM((T, block, 3 * block), BF),
            pltpu.VMEM((4 * block, T * LANES), BF),
            pltpu.VMEM((4 * block, T * LANES), BF),
            pltpu.VMEM((block, 4 * block), BF),
            pltpu.VMEM((block, 4 * block), BF),
            pltpu.VMEM((2 * LANES, LANES), BF),
            pltpu.VMEM((2 * LANES, LANES), BF),
            pltpu.VMEM((T, 2 * LANES, LANES), BF),
            pltpu.VMEM((T, 2 * LANES, LANES), BF),
            dma((SWEEPS, n - 1, chunks)),
            dma((SWEEPS, n - 1, chunks)),
            dma((SWEEPS, n - 1, chunks)),
            dma((SWEEPS, n - 1, chunks)),
            dma((SWEEPS, 2, T * width)),
            dma((SWEEPS, 2, T * width)),
            dma((1,)),
            dma((1,)),
            dma((4,)),
        ],
        compiler_params=pltpu.CompilerParams(
            collective_id=0, has_side_effects=True, vmem_limit_bytes=56 * 1024 * 1024
        ),
    )(flux_jac, jnp.asarray(node_matrices()), cross_nbr, lower_match, state, forcing, jacobi_inv)


def solution(mesh):
    n, ns = mesh.shape["inst"], mesh.shape["space"]
    return jax.shard_map(
        functools.partial(body, n, ns),
        mesh=mesh,
        in_specs=(
            P("inst", None, "space"),
            P("inst", None, "space"),
            P(),
            P("inst", None, None),
            P(),
            P("inst", "space", None),
        ),
        out_specs=(P("inst", None, "space"), P("inst", None, "space")),
        check_vma=False,
    )
```

```python
import functools
import math

import jax
import jax.numpy as jnp
import numpy as np
from jax import lax
from jax.experimental import pallas as pl
from jax.experimental.pallas import tpu as pltpu
from jax.sharding import PartitionSpec as P

NODE1 = 4
SWEEPS = 2
DISSIPATION = 0.6
FREQUENCY = 0.25
LANES = 128
MESH = pl.DeviceIdType.MESH
BF = jnp.bfloat16
F32 = jnp.float32


def lobatto_derivative(count_of_nodes):
    inner_point = math.sqrt(0.2)
    points = np.array([-1.0, -inner_point, inner_point, 1.0])
    bary = np.ones(count_of_nodes)
    for a in range(count_of_nodes):
        for b in range(count_of_nodes):
            if a != b:
                bary[a] = bary[a] / (points[a] - points[b])
    table = np.zeros((count_of_nodes, count_of_nodes))
    for a in range(count_of_nodes):
        for b in range(count_of_nodes):
            if a != b:
                table[a, b] = bary[b] / bary[a] / (points[a] - points[b])
        table[a, a] = -np.sum(table[a])
    return table


def node_matrices():
    n = NODE1
    scale = n * (n - 1) / 4.0
    der = lobatto_derivative(n).astype(np.float32).astype(np.float64)
    eye = np.eye(n)
    low, high = np.zeros((n, n)), np.zeros((n, n))
    low[0, 0] = 1.0
    high[n - 1, n - 1] = 1.0
    to_low, to_high = np.zeros((n, n)), np.zeros((n, n))
    to_low[0, n - 1] = 1.0
    to_high[n - 1, 0] = 1.0

    def place(m, d):
        parts = [eye, eye, eye]
        parts[d] = m
        return np.kron(np.kron(parts[0], parts[1]), parts[2])

    own = [place(der + scale * (low - high), d) for d in range(3)]
    own.append(DISSIPATION * scale * sum(place(low + high, d) for d in range(3)))
    for d in range(3):
        own.append(place(scale * (to_high - to_low), d))
        own.append(-DISSIPATION * scale * place(to_high + to_low, d))
    return np.stack(own).astype(np.float32)


def time_weights(count):
    half = count // 2
    d = np.zeros(count)
    for m in range(1, count):
        d[m] = 0.5 * FREQUENCY * (-1.0) ** m / math.tan(math.pi * m / count)
    d[half] = 0.0
    plus = np.zeros((half, half))
    minus = np.zeros((half, half))
    for t in range(half):
        for s in range(half):
            a, b = d[(t - s) % count], d[(t - s + half) % count]
            plus[t, s] = 0.5 * (a + b)
            minus[t, s] = 0.5 * (a - b)
    return plus, minus


def split(x):
    hi = x.astype(BF)
    return hi, (x - hi.astype(F32)).astype(BF)


def mm(a, b):
    return jnp.dot(a, b, preferred_element_type=F32)


def kernel(
    cfg, flux_hbm, nodes, cross, match, state_hbm, forcing_hbm, jac_hbm, res_hbm, upd_hbm,
    xbuf, ybuf, dbuf, halo, match_up, v1, spat, forc, jac, jcat, vh, vl, wh, wl, py, pz, pb, pa,
    flux, state, fsend, frecv, bsend, brecv, hsend, hrecv, msend, mrecv, lsem,
):
    n, ns, T, width, rows, arows, count, cells = cfg
    brows = rows - arows
    block = width * 64
    me = lax.axis_index("inst")
    sp = lax.axis_index("space")
    right, left = lax.rem(sp + 1, ns), lax.rem(sp + ns - 1, ns)
    offsets = sorted(range(1, n), key=lambda k: (-min(k, n - k), k))
    peers = [lax.rem(me + k, n) for k in offsets]

    load_s = pltpu.make_async_copy(state_hbm, state, lsem.at[3 + T])
    load_x = pltpu.make_async_copy(flux_hbm, flux, lsem.at[4 + T])
    load_s.start()
    load_x.start()
    load_f = pltpu.make_async_copy(forcing_hbm, forc, lsem.at[0])
    load_j = pltpu.make_async_copy(jac_hbm, jac, lsem.at[1])
    load_f.start()
    load_j.start()

    barrier = pltpu.get_barrier_semaphore()
    for p in peers:
        pl.semaphore_signal(barrier, inc=1, device_id={"inst": p}, device_id_type=MESH)
    for p in (right, left):
        pl.semaphore_signal(barrier, inc=1, device_id={"space": p}, device_id_type=MESH)
    pl.semaphore_wait(barrier, n + 1)
    load_s.wait()

    padded = n * rows != block
    exact0 = state
    if padded:
        for t in range(T):
            v1[0, t, 0:block, :] = state[t]
            v1[0, t, block:, :] = jnp.zeros((n * rows - block, LANES), F32)
            v1[1, t, block:, :] = jnp.zeros((n * rows - block, LANES), F32)
        exact0 = v1.at[0]

    def forward(sweep, src, k, c):
        p = peers[k]
        if c < T:
            t0, nt, r0, nr = c, 1, 0, arows
        else:
            t0, nt, r0, nr = 0, T, arows, brows
        return pltpu.make_async_remote_copy(
            src_ref=src.at[pl.ds(t0, nt), pl.ds(pl.multiple_of(p * rows + r0, 8), nr), :],
            dst_ref=xbuf.at[sweep, pl.ds(me * T + t0, nt), pl.ds(r0, nr), :],
            send_sem=fsend.at[sweep, k, c],
            recv_sem=frecv.at[sweep, k, c],
            device_id={"inst": p},
            device_id_type=MESH,
        )

    def backward(sweep, k, c):
        p = peers[k]
        if c < T:
            t0, nt, r0, nr = c, 1, arows, brows
        else:
            t0, nt, r0, nr = 0, T, 0, arows
        return pltpu.make_async_remote_copy(
            src_ref=ybuf.at[sweep, pl.ds(p * T + t0, nt), pl.ds(r0, nr), :],
            dst_ref=dbuf.at[sweep, pl.ds(t0, nt), pl.ds(pl.multiple_of(me * rows + r0, 8), nr), :],
            send_sem=bsend.at[sweep, k, c],
            recv_sem=brecv.at[sweep, k, c],
            device_id={"inst": p},
            device_id_type=MESH,
        )

    everyone = range(n - 1)

    def halos(sweep, src):
        out = []
        for t in range(T):
            for v in range(width):
                up = v * 64 + 48
                down = v * 64
                out.append(pltpu.make_async_remote_copy(
                    src_ref=src.at[t, pl.ds(up, 16), :],
                    dst_ref=halo.at[sweep, 0, t, pl.ds(v * 16, 16), :],
                    send_sem=hsend.at[sweep, 0, t * width + v],
                    recv_sem=hrecv.at[sweep, 0, t * width + v],
                    device_id={"space": right}, device_id_type=MESH))
                out.append(pltpu.make_async_remote_copy(
                    src_ref=src.at[t, pl.ds(down, 16), :],
                    dst_ref=halo.at[sweep, 1, t, pl.ds(v * 16, 16), :],
                    send_sem=hsend.at[sweep, 1, t * width + v],
                    recv_sem=hrecv.at[sweep, 1, t * width + v],
                    device_id={"space": left}, device_id_type=MESH))
        return out

    send_match = pltpu.make_async_remote_copy(
        src_ref=match, dst_ref=match_up, send_sem=msend.at[0], recv_sem=mrecv.at[0],
        device_id={"space": left}, device_id_type=MESH)

    plus, minus = time_weights(count)
    half = count // 2

    def derive(sweep, first, size):
        def group(g, _):
            at = pl.ds(pl.multiple_of(first + g * 8, 8), 8)
            low = [xbuf[sweep, s, at, :] for s in range(half)]
            high = [xbuf[sweep, s + half, at, :] for s in range(half)]
            sums = [a + b for a, b in zip(low, high)]
            diffs = [a - b for a, b in zip(low, high)]
            for t in range(half):
                acc, dif = None, None
                for s in range(half):
                    if abs(plus[t, s]) > 1e-12:
                        term = sums[s] * float(plus[t, s])
                        acc = term if acc is None else acc + term
                    if abs(minus[t, s]) > 1e-12:
                        term = diffs[s] * float(minus[t, s])
                        dif = term if dif is None else dif + term
                ybuf[sweep, t, at, :] = acc + dif
                ybuf[sweep, t + half, at, :] = acc - dif
            return 0
        lax.fori_loop(0, size // 8, group, 0)

    src_row = lax.broadcasted_iota(jnp.int32, (LANES, LANES), 0)
    dst_col = lax.broadcasted_iota(jnp.int32, (LANES, LANES), 1)

    def onehot(mask):
        return jnp.where(mask, 1.0, 0.0).astype(F32)

    def build_weights():
        lane_var = lax.broadcasted_iota(jnp.int32, (1, block), 1) // 64
        tiles = [jnp.concatenate([nodes[i]] * width, axis=1) for i in range(10)]
        for w in range(width):
            fe = []
            for d in range(3):
                row = jnp.zeros((1, block), F32)
                for v in range(width):
                    row = jnp.where(lane_var == v, flux[d, w:w + 1, v:v + 1], row)
                fe.append(row)
            same = jnp.where(lane_var == w, 1.0, 0.0)
            parts = [fe[0] * tiles[0] + fe[1] * tiles[1] + fe[2] * tiles[2] + same * tiles[3]]
            for d in range(3):
                parts.append(fe[d] * tiles[4 + 2 * d] + same * tiles[5 + 2 * d])
            hi, lo = split(jnp.concatenate(parts, axis=1))
            wh[w * 64:(w + 1) * 64, :] = hi
            wl[w * 64:(w + 1) * 64, :] = lo

    def build_moves():
        layer = (lax.broadcasted_iota(jnp.int32, (1, LANES), 1) // cells) * cells
        for f in range(4):
            nb = cross[f:f + 1, :]
            nb = jnp.concatenate([nb] * (LANES // cells), axis=1) + layer
            ref = py if f < 2 else pz
            ref[(f % 2) * LANES:(f % 2 + 1) * LANES, :] = onehot(src_row == nb).astype(BF)

    def build_match():
        last = LANES - cells
        low_ok = jnp.where(sp > 0, 1.0, 0.0)
        high_ok = jnp.where(sp < ns - 1, 1.0, 0.0)
        shift_up = onehot(dst_col == src_row + cells).astype(BF)
        shift_down = onehot(src_row == dst_col + cells).astype(BF)
        for t in range(T):
            m = jnp.concatenate([match[t]] * (LANES // cells), axis=1)
            mu = jnp.concatenate([match_up[t]] * (LANES // cells), axis=1)
            pb[t, 0:LANES, :] = shift_up
            pb[t, LANES:, :] = (onehot((dst_col < cells) & (src_row == m + last)) * low_ok).astype(BF)
            pa[t, 0:LANES, :] = shift_down
            turned = onehot((dst_col < cells) & (src_row == mu + last)) * high_ok
            pa[t, LANES:, :] = turned.T.astype(BF)

    row_id = lax.broadcasted_iota(jnp.int32, (block, 1), 0)

    def as_mask(index, value):
        return jnp.where(index == value, 1.0, 0.0).astype(F32)

    mj3, mj0 = as_mask((row_id >> 2) & 3, 3), as_mask((row_id >> 2) & 3, 0)
    mk3, mk0 = as_mask(row_id & 3, 3), as_mask(row_id & 3, 0)

    def spread_cross(src, t):
        cols = slice(t * LANES, (t + 1) * LANES)
        x = src[t, 0:block, :]
        for part, out in zip(split(x), (vh, vl)):
            out[0:block, cols] = part
            wide = part.astype(F32)
            y = jnp.concatenate([wide * mj3, wide * mj0], axis=1).astype(BF)
            z = jnp.concatenate([wide * mk3, wide * mk0], axis=1).astype(BF)
            out[2 * block:3 * block, cols] = mm(y, py[...]).astype(BF)
            out[3 * block:4 * block, cols] = mm(z, pz[...]).astype(BF)

    def spread_flow(sweep, src, t):
        cols = slice(t * LANES, (t + 1) * LANES)
        own_high = jnp.concatenate([src[t, v * 64 + 48:v * 64 + 64, :] for v in range(width)], axis=0)
        own_low = jnp.concatenate([src[t, v * 64:v * 64 + 16, :] for v in range(width)], axis=0)
        high = split(jnp.concatenate([own_high, halo[sweep, 0, t]], axis=1))
        low = split(jnp.concatenate([own_low, halo[sweep, 1, t]], axis=1))
        for i, out in enumerate((vh, vl)):
            ub = mm(high[i], pb[t]).astype(BF)
            ua = mm(low[i], pa[t]).astype(BF)
            for v in range(width):
                base = block + v * 64
                out[base:base + 16, cols] = ua[v * 16:(v + 1) * 16]
                out[base + 48:base + 64, cols] = ub[v * 16:(v + 1) * 16]

    def clear_middle():
        for out in (vh, vl):
            for v in range(width):
                base = block + v * 64 + 16
                out[base:base + 32, :] = jnp.zeros((32, T * LANES), BF)

    def split_jac():
        load_j.wait()
        for t in range(T):
            hi, lo = split(jac[t])
            jcat[t] = jnp.concatenate([hi, lo, hi], axis=1)

    def apply_space():
        total = mm(wh[...], vh[...]) + mm(wl[...], vh[...]) + mm(wh[...], vl[...])
        for t in range(T):
            spat[t] = total[:, t * LANES:(t + 1) * LANES] - forc[t]

    own_rows = pl.ds(pl.multiple_of(me * rows, 8), rows)
    own_times = pl.ds(me * T, T)

    def run_sweep(sweep, src, before, between):
        xbuf[sweep, own_times, :, :] = src[:, own_rows, :]
        for job in before:
            job()
        for c in range(T):
            for k in everyone:
                forward(sweep, src, k, c).wait_recv()
        derive(sweep, 0, arows)
        for k in everyone:
            backward(sweep, k, T).start()
        for job in between:
            job()
        for k in everyone:
            forward(sweep, src, k, T).wait_recv()
        derive(sweep, arows, brows)
        for c in range(T):
            for k in everyone:
                backward(sweep, k, c).start()
        dbuf[sweep, :, own_rows, :] = ybuf[sweep, own_times, :, :]

    def finish(sweep, src, dst, after):
        for k in everyone:
            backward(sweep, k, T).wait_recv()
        for t in range(T):
            for k in everyone:
                backward(sweep, k, t).wait_recv()
            r = spat[t] + dbuf[sweep, t, 0:block, :]
            if sweep == 0:
                spat[t] = r
            hi, lo = split(r)
            step = mm(jcat[t], jnp.concatenate([hi, hi, lo], axis=0))
            dst[t, 0:block, :] = src[t, 0:block, :] - step
            after(t)

    def send_forward(sweep, src, c):
        for k in everyone:
            forward(sweep, src, k, c).start()

    def wait_halos(sweep, src):
        for h in halos(sweep, src):
            h.wait_recv()

    def first_halo_ready():
        send_match.wait()
        wait_halos(0, state)
        build_match()

    for c in range(T + 1):
        send_forward(0, exact0, c)
    send_match.start()
    for h in halos(0, state):
        h.start()
    before = [build_moves, load_x.wait, build_weights]
    before += [functools.partial(spread_cross, state, t) for t in range(T)]
    before += [clear_middle]
    between = [first_halo_ready]
    between += [functools.partial(spread_flow, 0, state, t) for t in range(T)]
    between += [load_f.wait, apply_space, split_jac]
    run_sweep(0, exact0, before, between)
    cur = v1.at[1]
    finish(0, state, cur, lambda t: send_forward(1, cur, t))

    send_forward(1, cur, T)
    for h in halos(1, cur):
        h.start()
    store_r = pltpu.make_async_copy(spat, res_hbm, lsem.at[2])
    store_r.start()
    before = [functools.partial(spread_cross, cur, t) for t in range(T)]
    between = [functools.partial(wait_halos, 1, cur)]
    between += [functools.partial(spread_flow, 1, cur, t) for t in range(T)]
    between += [store_r.wait, apply_space]
    run_sweep(1, cur, before, between)
    stores = [pltpu.make_async_copy(forc.at[t], upd_hbm.at[t], lsem.at[3 + t]) for t in range(T)]
    finish(1, cur, forc, lambda t: stores[t].start())
    for sweep, src in ((0, exact0), (1, cur)):
        for c in range(T + 1):
            for k in everyone:
                forward(sweep, src, k, c).wait_send()
                backward(sweep, k, c).wait_send()
        for h in halos(sweep, state if sweep == 0 else cur):
            h.wait_send()
    for store in stores:
        store.wait()


def body(n, ns, state, forcing, flux_jac, jacobi_inv, cross_nbr, lower_match):
    T, block, elements = state.shape
    width = flux_jac.shape[1]
    cells = cross_nbr.shape[1]
    count = n * T
    rows = -(-block // (8 * n)) * 8
    arows = -(-rows // 16) * 8
    pieces = T + 1
    halo_rows = width * 16
    cfg = (n, ns, T, width, rows, arows, count, cells)
    full = n * rows
    dma = pltpu.SemaphoreType.DMA
    vmem = pl.BlockSpec(memory_space=pltpu.VMEM)
    hbm = pl.BlockSpec(memory_space=pl.ANY)
    out = jax.ShapeDtypeStruct(state.shape, F32)
    return pl.pallas_call(
        functools.partial(kernel, cfg),
        name="sweeps",
        out_shape=(out, out),
        in_specs=[hbm, vmem, vmem, vmem, hbm, hbm, hbm],
        out_specs=(hbm, hbm),
        scratch_shapes=[
            pltpu.VMEM((SWEEPS, count, rows, LANES), F32),
            pltpu.VMEM((SWEEPS, count, rows, LANES), F32),
            pltpu.VMEM((SWEEPS, T, full, LANES), F32),
            pltpu.VMEM((SWEEPS, 2, T, halo_rows, LANES), F32),
            pltpu.VMEM((T, 1, cells), jnp.int32),
            pltpu.VMEM((2, T, full, LANES), F32),
            pltpu.VMEM((T, block, LANES), F32),
            pltpu.VMEM((T, block, LANES), F32),
            pltpu.VMEM((T, block, block), F32),
            pltpu.VMEM((T, block, 3 * block), BF),
            pltpu.VMEM((4 * block, T * LANES), BF),
            pltpu.VMEM((4 * block, T * LANES), BF),
            pltpu.VMEM((block, 4 * block), BF),
            pltpu.VMEM((block, 4 * block), BF),
            pltpu.VMEM((2 * LANES, LANES), BF),
            pltpu.VMEM((2 * LANES, LANES), BF),
            pltpu.VMEM((T, 2 * LANES, LANES), BF),
            pltpu.VMEM((T, 2 * LANES, LANES), BF),
            pltpu.VMEM(flux_jac.shape, F32),
            pltpu.VMEM((T, block, LANES), F32),
            dma((SWEEPS, n - 1, pieces)),
            dma((SWEEPS, n - 1, pieces)),
            dma((SWEEPS, n - 1, pieces)),
            dma((SWEEPS, n - 1, pieces)),
            dma((SWEEPS, 2, T * width)),
            dma((SWEEPS, 2, T * width)),
            dma((1,)),
            dma((1,)),
            dma((5 + T,)),
        ],
        compiler_params=pltpu.CompilerParams(
            collective_id=0, has_side_effects=True, vmem_limit_bytes=56 * 1024 * 1024
        ),
    )(flux_jac, jnp.asarray(node_matrices()), cross_nbr, lower_match, state, forcing, jacobi_inv)


def solution(mesh):
    n, ns = mesh.shape["inst"], mesh.shape["space"]
    return jax.shard_map(
        functools.partial(body, n, ns),
        mesh=mesh,
        in_specs=(
            P("inst", None, "space"),
            P("inst", None, "space"),
            P(),
            P("inst", None, None),
            P(),
            P("inst", "space", None),
        ),
        out_specs=(P("inst", None, "space"), P("inst", None, "space")),
        check_vma=False,
    )
```
